128 devices in a mesh: region: 8 (over y, core), seq: 16 (over z, x).
Axes of the slice: x: 4, y: 4, z: 4, core: 2. Of those that a mesh axis runs over, the one named last changes fastest.
Arguments:
- scan_tokens: bfloat16 [131072, 1024], P(('region', 'seq')), may hold values from -6 to 6
- grid_tokens: bfloat16 [32768, 1024], P(('region', 'seq')), may hold values from -6 to 6
- seg_slot: int32 [1024], P(('region', 'seq')), may hold values from 0 to 1023, as said below
- segment_lists: int32 [256, 8], P(('region', 'seq')), may hold values from 0 to 1023, as said below
- query_weight: bfloat16 [1024, 1024], replicated, may hold values from -4 to 4
- key_weight: bfloat16 [1024, 1024], replicated, may hold values from -4 to 4
- value_weight: bfloat16 [1024, 1024], replicated, may hold values from -0.1875 to 0.1875
- mixer_weight: bfloat16 [1024, 1024], replicated, may hold values from -0.1875 to 0.1875
- packed_weight: bfloat16 [1024, 3072], replicated, may hold values from -4 to 4
- merged_weight: bfloat16 [1024, 1024], replicated, may hold values from -0.1875 to 0.1875
Outputs:
- encoded: bfloat16 [32768, 1024], P(('region', 'seq'))
The draws below stay inside these ranges and needn't reach their ends.
Inputs may be any that keep to these rules, and one draw needn't show every extreme that they name: `seg_slot`: A permutation: each of the 1024 segment slots holds exactly one segment. `segment_lists`: the 8 segments of a query block are held by 8 different devices, all of the block's own region (the devices that share the block's device's index along region); so the blocks of one device name at most 2 segments held by any one device, and in every draw and every region some device holds a segment of every query block of that region.
All inputs are finite; a program needn't handle non-finite values.
Results may differ from the reference program's by a relative error of at most 0.01.
The reference program's roundings to bfloat16 on the way count: a program that leaves them out, or rounds other values in their place, can miss the bound.
Values may be sent and summed in bfloat16 or wider, within the bound.
No kernel may reach another device: no remote copies, remote signals or barrier semaphores. Data moves between devices by JAX's collectives and lax.ppermute only.
A program may use at most 128 MiB of HBM per device.

```python
import math
import jax
import jax.numpy as jnp
from jax import lax

D = 1024
H = 16
HD = 64
SEG = 128
QB = 128
OV = 8
QPD = 2
SPD = 8
NS = 131072
NG = 32768
NSEG = 1024
NQB = 256
RL = 4096
N_REGION = 8
N_SEQ = 16


def layout_tables(key):
    seeded = jax.random.fold_in(key, 7101)
    key_perm, key_busy, key_popular, key_drawn, key_local, key_order = jax.random.split(seeded, 6)
    permuted = jax.random.permutation(key_perm, NSEG).astype(jnp.int32)
    inverse = jnp.argsort(permuted).astype(jnp.int32)
    heaviest_target = jax.random.randint(key_busy, (N_REGION, 1, 1, 1), 0, N_SEQ)
    frequent_targets = jax.random.randint(key_popular, (N_REGION, 1, 1, N_SEQ), 0, 1 << 20)
    sampled_picks = jax.random.randint(key_drawn, (N_REGION, N_SEQ, QPD, N_SEQ), 0, 1 << 20)
    destination_index = jnp.arange(N_SEQ, dtype=jnp.int32)
    extra_score_term = jnp.where(destination_index[None, None, None, :] == heaviest_target, 1 << 22, 0)
    logit_scores = (sampled_picks + frequent_targets + extra_score_term) * N_SEQ + destination_index[None, None, None, :]
    top_values, chosen = lax.top_k(logit_scores, OV)
    order_keys = jax.random.randint(key_order, (N_REGION, N_SEQ, QPD, OV), 0, 1 << 20) * OV + jnp.arange(OV, dtype=jnp.int32)
    shuffle = jnp.argsort(order_keys, axis=-1)
    chosen = jnp.take_along_axis(chosen, shuffle, axis=-1).astype(jnp.int32)
    local_slot = jax.random.randint(key_local, (N_REGION, N_SEQ, QPD, OV), 0, SPD)
    region_ids = jnp.arange(N_REGION, dtype=jnp.int32)[:, None, None, None]
    target = (region_ids * N_SEQ + chosen) * SPD + local_slot
    listed = jnp.take(inverse, target.reshape(NQB, OV), axis=0).astype(jnp.int32)
    return (permuted, listed)


def draw_seg_slot(key, part):
    return layout_tables(key)[0]


def draw_segment_lists(key, part):
    return layout_tables(key)[1]


def clipped_normal(key, dims):
    return jnp.clip(jax.random.normal(key, dims, dtype=jnp.float32), -6.0, 6.0) / math.sqrt(D)


def cross_pair(key):
    seeded = jax.random.fold_in(key, 7202)
    key_first, key_second = jax.random.split(seeded, 2)
    first = clipped_normal(key_first, (D, D))
    second = clipped_normal(key_second, (D, D))
    return (jnp.clip(first, -4.0, 4.0), jnp.clip(second, -4.0, 4.0))


def draw_query_weight(key, part):
    return cross_pair(key)[0].astype(jnp.bfloat16)


def draw_key_weight(key, part):
    return cross_pair(key)[1].astype(jnp.bfloat16)


def draw_packed_weight(key, part):
    seeded = jax.random.fold_in(key, 7303)
    key_query, key_keys, key_values = jax.random.split(seeded, 3)
    query_part = clipped_normal(key_query, (D, H, HD))
    value_part = clipped_normal(key_values, (D, H, HD))
    key_part = clipped_normal(key_keys, (D, H, HD))
    stacked = jnp.stack([query_part, key_part, value_part], axis=2).reshape(D, 3 * D)
    return jnp.clip(stacked, -4.0, 4.0).astype(jnp.bfloat16)


def shard_levels(rng, extent, cuts, low, high):
    loudness = 1.0
    for dim, shards_of in cuts:
        heights = jax.random.uniform(jax.random.fold_in(jax.random.fold_in(rng, 6), dim), (shards_of,), jnp.float32, low / len(cuts), high / len(cuts))
        loudness = loudness * jnp.repeat(jnp.exp(heights), extent[dim] // shards_of).reshape((-1,) + (1,) * (len(extent) - 1 - dim))
    return loudness


def normal_values(rng, shape, deviation, bound, shards=(), kind=jnp.bfloat16):
    drawn = jax.random.normal(rng, shape, jnp.float32) * deviation
    if len(shards) > 0:
        drawn = shard_levels(rng, shape, shards, -0.22, 0.18) * drawn
    return jnp.clip(drawn, min=-bound, max=bound).astype(kind)


def setup_inputs(seed: int = 0) -> dict:
    arg_keys = jax.random.split(jax.random.key(seed), 11)
    return {
        "scan_tokens": normal_values(arg_keys[0], (NS, D), 1.0, 6.0, ((0, 128),)),
        "grid_tokens": normal_values(arg_keys[1], (NG, D), 1.0, 6.0, ((0, 128),)),
        "seg_slot": draw_seg_slot(jax.random.fold_in(arg_keys[10], 71), 0),
        "segment_lists": draw_segment_lists(jax.random.fold_in(arg_keys[10], 71), 0),
        "query_weight": draw_query_weight(jax.random.fold_in(arg_keys[10], 71), 0),
        "key_weight": draw_key_weight(jax.random.fold_in(arg_keys[10], 71), 0),
        "value_weight": normal_values(arg_keys[6], (D, D), D ** -0.5, 0.1875),
        "mixer_weight": normal_values(arg_keys[7], (D, D), D ** -0.5, 0.1875),
        "packed_weight": draw_packed_weight(jax.random.fold_in(arg_keys[10], 71), 0),
        "merged_weight": normal_values(arg_keys[9], (D, D), D ** -0.5, 0.1875),
    }


norm_eps = 1e-06
masked_score = -1e+30

def rms_rows(values):
    widened = values.astype(jnp.float32)
    scaled = widened / jnp.sqrt(lax.optimization_barrier(jnp.mean(widened * widened, axis=-1, keepdims=True)) + norm_eps)
    return scaled.astype(jnp.bfloat16)

def pair_partials(queries, seg_keys, seg_values, head_count):
    pair_count, query_rows, model_width = queries.shape
    key_rows = seg_keys.shape[1]
    head_dim = model_width // head_count
    q_split = queries.reshape(pair_count, query_rows, head_count, head_dim).astype(jnp.float32)
    k_split = seg_keys.reshape(pair_count, key_rows, head_count, head_dim).astype(jnp.float32)
    v_split = seg_values.reshape(pair_count, key_rows, head_count, head_dim).astype(jnp.float32)
    logit_scores = jnp.einsum('bqhd,bkhd->bhqk', q_split, k_split) * (1.0 / math.sqrt(head_dim))
    maxima = lax.optimization_barrier(jnp.max(logit_scores, axis=-1))
    weights = jnp.exp(logit_scores - maxima[..., None])
    running_sums = lax.optimization_barrier(jnp.sum(weights, axis=-1))
    rounded = lax.optimization_barrier(weights.astype(jnp.bfloat16)).astype(jnp.float32)
    numerator = jnp.einsum('bhqk,bkhd->bqhd', rounded, v_split)
    return (numerator.reshape(pair_count, query_rows, model_width), maxima, running_sums)

def joined_pair_list(numerator, maxima, running_sums, live_pairs, head_count):
    live_mask = live_pairs[:, :, None, None]
    maxima = jnp.where(live_mask, maxima, masked_score)
    top_score = lax.optimization_barrier(jnp.max(maxima, axis=0))
    factors = jnp.where(live_mask, jnp.exp(maxima - top_score[None]), 0.0)
    denominator = lax.optimization_barrier(jnp.sum(factors * running_sums, axis=0))
    pair_count, block_count, query_rows, model_width = numerator.shape
    split_heads = numerator.reshape(pair_count, block_count, query_rows, head_count, model_width // head_count)
    summed = lax.optimization_barrier(jnp.sum(split_heads * jnp.swapaxes(factors, 2, 3)[..., None], axis=0))
    merged = summed / jnp.swapaxes(denominator, 1, 2)[..., None]
    return merged.reshape(block_count, query_rows, model_width).astype(jnp.bfloat16)

def region_attention(packed, heads_local, head_dim):
    row_count = packed.shape[0]
    queries = packed[:, :, 0].astype(jnp.float32)
    head_keys = packed[:, :, 1].astype(jnp.float32)
    head_values = packed[:, :, 2].astype(jnp.float32)
    step_rows = min(512, row_count)

    def one_block(query_part):
        logit_scores = jnp.einsum('qhd,khd->hqk', query_part, head_keys) * (1.0 / math.sqrt(head_dim))
        maxima = lax.optimization_barrier(jnp.max(logit_scores, axis=-1, keepdims=True))
        weights = jnp.exp(logit_scores - maxima)
        running_sums = lax.optimization_barrier(jnp.sum(weights, axis=-1))
        rounded = lax.optimization_barrier(weights.astype(jnp.bfloat16)).astype(jnp.float32)
        numerator = jnp.einsum('hqk,khd->qhd', rounded, head_values)
        return (numerator / jnp.transpose(running_sums)[..., None]).astype(jnp.bfloat16)
    blocks = lax.map(one_block, queries.reshape(row_count // step_rows, step_rows, heads_local, head_dim))
    return blocks.reshape(row_count, heads_local * head_dim)

def reference(scan_tokens, grid_tokens, seg_slot, segment_lists, query_weight, key_weight, value_weight, mixer_weight, packed_weight, merged_weight):
    scan_normed = rms_rows(scan_tokens)
    all_keys = jnp.dot(scan_normed, key_weight, preferred_element_type=jnp.float32).astype(jnp.bfloat16)
    all_values = jnp.dot(scan_normed, value_weight, preferred_element_type=jnp.float32).astype(jnp.bfloat16)
    queries = jnp.dot(rms_rows(grid_tokens), query_weight, preferred_element_type=jnp.float32).astype(jnp.bfloat16)
    queries = queries.reshape(NQB, QB, D)
    slots = jnp.take(seg_slot, segment_lists, axis=0).astype(jnp.int32)
    offsets = jnp.arange(SEG, dtype=jnp.int32)

    def one_block(element):
        block_queries, slot_row = element
        row_ids = (slot_row[:, None] * SEG + offsets[None, :]).astype(jnp.int32)
        seg_keys = jnp.take(all_keys, row_ids, axis=0)
        seg_values = jnp.take(all_values, row_ids, axis=0)
        spread = jnp.broadcast_to(block_queries[None], (OV, QB, D))
        numerator, maxima, running_sums = pair_partials(spread, seg_keys, seg_values, H)
        live_pairs = jnp.ones((OV, 1), dtype=bool)
        return joined_pair_list(numerator[:, None], maxima[:, None], running_sums[:, None], live_pairs, H)[0]
    cross = lax.map(one_block, (queries, slots)).reshape(NG, D)
    mixed = (grid_tokens.astype(jnp.float32) + jnp.dot(cross, mixer_weight, preferred_element_type=jnp.float32)).astype(jnp.bfloat16)
    packed = jnp.dot(rms_rows(mixed), packed_weight, preferred_element_type=jnp.float32).astype(jnp.bfloat16)
    packed = packed.reshape(N_REGION, RL, H, 3, HD)

    def one_region(region_packed):
        per_head = jnp.transpose(region_packed, (1, 0, 2, 3))[:, :, None]
        outputs = lax.map(lambda head_packed: region_attention(head_packed, 1, HD), per_head)
        return jnp.transpose(outputs, (1, 0, 2)).reshape(RL, H * HD)
    attended = lax.map(one_region, packed).reshape(NG, D)
    return (mixed.astype(jnp.float32) + jnp.dot(attended, merged_weight, preferred_element_type=jnp.float32)).astype(jnp.bfloat16)
```

```python
import functools
import math

import jax
import jax.numpy as jnp
from jax import lax
from jax.experimental import pallas as pl
from jax.experimental.pallas import tpu as pltpu
from jax.sharding import PartitionSpec as P


AX = ("region", "seq")
D = 1024
H = 16
SEG = 128
PAIRS = 8
EPS = 1e-06
DEAD = -1e30
SCALE = (1.0 / math.sqrt(64)) * math.log2(math.e)
WIRE = D + 128
BF = jnp.bfloat16
F32 = jnp.float32
ANY = pl.BlockSpec(memory_space=pl.ANY)
SMEM = pl.BlockSpec(memory_space=pltpu.SMEM)
VMEM = pl.BlockSpec(memory_space=pltpu.VMEM)


def ring(mesh_shape, along_first, step):
    regions, rows, cols = mesh_shape
    pairs = []
    for r in range(regions):
        for z in range(rows):
            for x in range(cols):
                if (r % 2 == 0) == along_first:
                    dest = (r, (z + step) % rows, x)
                else:
                    dest = (r, z, (x + step) % cols)
                pairs.append(
                    ((r * rows + z) * cols + x, (dest[0] * rows + dest[1]) * cols + dest[2])
                )
    return pairs


def normed(rows):
    wide = rows.astype(F32)
    inv = 1.0 / jnp.sqrt(jnp.mean(wide * wide, axis=-1, keepdims=True) + EPS)
    return (wide * inv).astype(BF)


def low_lanes(rows):
    return lax.broadcasted_iota(jnp.int32, (rows, 128), 1) < 64


def plan_kernel(where_ref, meta_ref, plan_ref):
    region, a, b = where_ref[0], where_ref[1], where_ref[2]
    odd = region % 2

    def clear(n, _):
        plan_ref[n] = -1
        return 0

    lax.fori_loop(0, 128, clear, 0)
    for c in range(4):
        plan_ref[64 + c] = 0

    def look(n, _):
        block = n // 8
        peer_b = (b + block // 2) % 4
        seq = jnp.where(odd == 0, a * 4 + peer_b, peer_b * 4 + a)
        seg = meta_ref[region * 16 + seq, 8 + n % 16]
        slot = meta_ref[seg // 8, seg % 8] - region * 128
        owner = slot // 8
        first, second = owner // 4, owner % 4
        owner_a = jnp.where(odd == 0, first, second)
        owner_b = jnp.where(odd == 0, second, first)
        local = slot % 8
        c = (owner_a - a + 4) % 4

        @pl.when(owner_b == b)
        def _():
            seen = plan_ref[72 + c * 8 + local]

            @pl.when(seen < 0)
            def _():
                count = plan_ref[64 + c]
                plan_ref[72 + c * 8 + local] = count
                plan_ref[32 + c * 8 + count] = local
                plan_ref[64 + c] = count + 1

            plan_ref[c * 8 + block] = plan_ref[72 + c * 8 + local]

        return 0

    lax.fori_loop(0, 64, look, 0)


def make_plan(where, meta):
    return pl.pallas_call(
        plan_kernel,
        out_shape=jax.ShapeDtypeStruct((128,), jnp.int32),
        in_specs=[SMEM, SMEM],
        out_specs=SMEM,
        name="plan",
    )(where, meta)


def cross_kernel(chunks, halves, first, *refs):
    chunk_count = len(chunks)
    plan = refs[0]
    q_in = refs[1:5]
    at = 5
    x_in = []
    for h in halves:
        x_in.append(refs[at : at + h])
        at += h
    wk, wv = refs[at : at + 2]
    at += 2
    state = None
    if not first:
        state = refs[at : at + 3]
        at += 3
        outs = refs[at : at + 4]
        at += 4
        num, top, tot = refs[at : at + 3]
        at += 3
    else:
        num, top, tot = refs[at : at + 3]
        at += 3
    q_all, xg, kb, vb, qsem, xsem = refs[at:]
    step = pl.program_id(0)

    def x_copy(j, n, part):
        c = chunks[j]
        seg = plan[32 + c * 8 + n]
        rows = SEG * 8 // halves[j]
        start = pl.multiple_of(seg * SEG - part * rows, SEG)
        return pltpu.make_async_copy(
            x_in[j][part].at[pl.ds(start, SEG), :], xg.at[j * 8 + n], xsem.at[j * 8 + n]
        )

    @pl.when(step == 0)
    def _():
        for j in range(chunk_count):
            c = chunks[j]

            def begin(n, _, j=j, c=c):
                if halves[j] == 1:
                    x_copy(j, n, 0).start()
                else:
                    low = plan[32 + c * 8 + n] < 4

                    @pl.when(low)
                    def _():
                        x_copy(j, n, 0).start()

                    @pl.when(jnp.logical_not(low))
                    def _():
                        x_copy(j, n, 1).start()

                return 0

            lax.fori_loop(0, plan[64 + c], begin, 0)
        for p in range(4):
            pltpu.make_async_copy(q_in[p], q_all.at[p], qsem.at[p]).start()
        for j in range(chunk_count):
            c = chunks[j]
            count = plan[64 + c]

            def finish(n, _, j=j):
                pltpu.make_async_copy(
                    x_in[j][0].at[pl.ds(0, SEG), :], xg.at[j * 8 + n], xsem.at[j * 8 + n]
                ).wait()
                return 0

            lax.fori_loop(0, count, finish, 0)

            def project(i, _, j=j):
                at_slot = j * 8 + 2 * i
                rows = normed(xg[pl.ds(at_slot, 2)].reshape(2 * SEG, D))
                keys = jnp.dot(rows, wk[...], preferred_element_type=F32).astype(BF)
                kb[pl.ds(at_slot, 2)] = keys.reshape(2, SEG, D)
                values = jnp.dot(rows, wv[...], preferred_element_type=F32).astype(BF)
                vb[pl.ds(at_slot, 2)] = values.reshape(2, SEG, D)
                return 0

            lax.fori_loop(0, (count + 1) // 2, project, 0)
        for p in range(4):
            pltpu.make_async_copy(q_in[p], q_all.at[p], qsem.at[p]).wait()

    if first:
        num[...] = jnp.zeros_like(num)
        tot[...] = jnp.zeros_like(tot)
        top[...] = jnp.full_like(top, DEAD)
    else:
        num[...] = state[0][...]
        top[...] = state[1][...]
        tot[...] = state[2][...]

    low = low_lanes(SEG)
    ones = jnp.ones((SEG, 128), BF)
    zeros = jnp.zeros((SEG, 128), BF)
    ones_low = jnp.where(low, ones, zeros)
    ones_high = jnp.where(low, zeros, ones)
    peer, half = step // 2, step % 2

    for j in range(chunk_count):
        pos = plan[chunks[j] * 8 + step]

        @pl.when(pos >= 0)
        def _(j=j, pos=pos):
            def one_pair(hp, _):
                del _
                lanes = pl.ds(hp * 128, 128)
                q = q_all[peer, pl.ds(pl.multiple_of(half * SEG, SEG), SEG), lanes]
                k = kb[j * 8 + pos, :, lanes]
                v = vb[j * 8 + pos, :, lanes]
                k2 = jnp.concatenate([jnp.where(low, k, zeros), jnp.where(low, zeros, k)], axis=0)
                s = lax.dot_general(
                    q, k2, (((1,), (1,)), ((), ())), preferred_element_type=F32
                )
                sa, sb = s[:, :128], s[:, 128:]
                ma = jnp.max(sa, axis=-1, keepdims=True)
                mb = jnp.max(sb, axis=-1, keepdims=True)
                pa = jnp.exp2((sa - ma) * SCALE).astype(BF)
                pb = jnp.exp2((sb - mb) * SCALE).astype(BF)
                v2 = jnp.concatenate(
                    [
                        jnp.concatenate([jnp.where(low, v, zeros), ones_low], axis=1),
                        jnp.concatenate([jnp.where(low, zeros, v), ones_high], axis=1),
                    ],
                    axis=0,
                )
                out = jnp.dot(
                    jnp.concatenate([pa, pb], axis=1), v2, preferred_element_type=F32
                )
                m_pair = jnp.where(low, ma, mb)
                m_old = top[:, lanes]
                m_new = jnp.maximum(m_old, m_pair)
                keep = jnp.exp2((m_old - m_new) * SCALE)
                add = jnp.exp2((m_pair - m_new) * SCALE)
                top[:, lanes] = m_new
                num[:, lanes] = num[:, lanes] * keep + out[:, :128] * add
                tot[:, lanes] = tot[:, lanes] * keep + out[:, 128:] * add

            for hp in range(PAIRS):
                one_pair(hp, 0)

    if not first:
        lane = lax.broadcasted_iota(jnp.int32, (SEG, 128), 1)
        which = (lane // 8) % 8
        stat = jnp.zeros((SEG, 128), F32)
        for hp in range(PAIRS):
            lanes = pl.ds(hp * 128, 128)
            mine = jnp.where(which < 4, top[:, lanes], tot[:, lanes])
            stat = jnp.where(lane % 8 == hp, mine, stat)
        hi = stat.astype(BF)
        rest = stat - hi.astype(F32)
        mid = rest.astype(BF)
        rest = rest - mid.astype(F32)
        part = which % 4
        picked = jnp.where(part == 0, hi.astype(F32), jnp.where(part == 1, mid.astype(F32), rest))
        picked = jnp.where(part == 3, 0.0, picked).astype(BF)
        sums = num[...].astype(BF)
        for p in range(4):

            @pl.when(peer == p)
            def _(p=p):
                outs[p][:, pl.ds(0, D)] = sums
                outs[p][:, pl.ds(D, 128)] = picked


def cross_call(plan, queries, chunks, tokens, wk, wv, state=None):
    first = state is None
    halves = [len(t) for t in tokens]
    flat = [part for t in tokens for part in t]
    rows = 8 * SEG
    block = pl.BlockSpec((SEG, D), lambda i: (i, 0))
    whole = pl.BlockSpec((D, D), lambda i: (0, 0), pipeline_mode=pl.Buffered(1))
    in_specs = [SMEM] + [ANY] * (4 + len(flat)) + [whole, whole]
    n = len(chunks)
    slots = [
        pltpu.VMEM((4, 2 * SEG, D), BF),
        pltpu.VMEM((n * 8, SEG, D), BF),
        pltpu.VMEM((n * 8, SEG, D), BF),
        pltpu.VMEM((n * 8, SEG, D), BF),
        pltpu.SemaphoreType.DMA((4,)),
        pltpu.SemaphoreType.DMA((n * 8,)),
    ]
    if first:
        out_shape = [jax.ShapeDtypeStruct((rows, D), F32)] * 3
        out_specs = [block] * 3
        scratch = slots
        args = ()
    else:
        in_specs += [block] * 3
        out_shape = [jax.ShapeDtypeStruct((2 * SEG, WIRE), BF)] * 4
        out_specs = [
            pl.BlockSpec((SEG, WIRE), lambda i, p=p: (jnp.clip(i - 2 * p, 0, 1), 0))
            for p in range(4)
        ]
        scratch = [pltpu.VMEM((SEG, D), F32)] * 3 + slots
        args = tuple(state)
    return pl.pallas_call(
        functools.partial(cross_kernel, chunks, halves, first),
        grid=(8,),
        out_shape=out_shape,
        in_specs=in_specs,
        out_specs=out_specs,
        scratch_shapes=scratch,
        compiler_params=pltpu.CompilerParams(vmem_limit_bytes=56 << 20),
        cost_estimate=pl.CostEstimate(
            flops=n * 8 * 700_000_000, bytes_accessed=20 << 20, transcendentals=n * 8 * 300_000
        ),
        name="cross_first" if first else "cross_last",
    )(plan, *queries, *flat, wk, wv, *args)


def home_kernel(p0, p1, p2, p3, grid_ref, wm_hbm, wp_hbm, mixed_ref, wire_ref, wm, wp, sems):
    wm_copy = pltpu.make_async_copy(wm_hbm, wm, sems.at[0])
    wp_copy = pltpu.make_async_copy(wp_hbm, wp, sems.at[1])
    wm_copy.start()
    wp_copy.start()
    parts = (p0, p1, p2, p3)
    rows = 2 * SEG
    lane = lax.broadcasted_iota(jnp.int32, (128, D), 0)
    col = lax.broadcasted_iota(jnp.int32, (128, D), 1)
    head = 2 * (lane % 8) + lane // 64
    which = (lane // 8) % 8
    hit = head == col // 64
    to_top = jnp.where(hit & (which < 3), 1.0, 0.0).astype(BF)
    to_tot = jnp.where(hit & (which >= 4) & (which < 7), 1.0, 0.0).astype(BF)
    tops = [jnp.dot(p[:, pl.ds(D, 128)], to_top, preferred_element_type=F32) for p in parts]
    tots = [jnp.dot(p[:, pl.ds(D, 128)], to_tot, preferred_element_type=F32) for p in parts]
    best = jnp.maximum(jnp.maximum(tops[0], tops[1]), jnp.maximum(tops[2], tops[3]))
    upper = jnp.zeros((rows, D), F32)
    lower = jnp.zeros((rows, D), F32)
    for p, m, t in zip(parts, tops, tots):
        factor = jnp.exp2((m - best) * SCALE)
        upper += factor * p[:, pl.ds(0, D)].astype(F32)
        lower += factor * t
    cross = (upper / lower).astype(BF)
    wm_copy.wait()
    mixed = (
        grid_ref[...].astype(F32) + jnp.dot(cross, wm[...], preferred_element_type=F32)
    ).astype(BF)
    mixed_ref[...] = mixed
    ready = normed(mixed)
    wp_copy.wait()
    low = low_lanes(rows)
    low_half = low_lanes(SEG)
    for hp in range(PAIRS):
        t = jnp.dot(ready, wp[:, pl.ds(hp * 384, 384)], preferred_element_type=F32)
        t = t.astype(BF).astype(F32)
        t0, t1, t2 = t[:, :128], t[:, 128:256], t[:, 256:]
        wire_ref[2 * hp, pl.ds(0, rows), :] = t0.astype(BF)
        wire_ref[2 * hp + 1, pl.ds(0, rows), :] = pltpu.roll(
            jnp.where(low, t2, t1), 64, 1
        ).astype(BF)
        wire_ref[2 * hp, pl.ds(rows, SEG), :] = jnp.where(
            low_half, t1[:SEG], pltpu.roll(t1[SEG:], 64, 1)
        ).astype(BF)
        wire_ref[2 * hp + 1, pl.ds(rows, SEG), :] = jnp.where(
            low_half, pltpu.roll(t2[:SEG], 64, 1), t2[SEG:]
        ).astype(BF)


def home_call(parts, grid_tokens, wm, wp):
    return pl.pallas_call(
        home_kernel,
        out_shape=[
            jax.ShapeDtypeStruct((2 * SEG, D), BF),
            jax.ShapeDtypeStruct((H, 3 * SEG, 128), BF),
        ],
        in_specs=[VMEM] * 5 + [ANY, ANY],
        out_specs=[VMEM, VMEM],
        scratch_shapes=[
            pltpu.VMEM((D, D), BF),
            pltpu.VMEM((D, 3 * D), BF),
            pltpu.SemaphoreType.DMA((2,)),
        ],
        compiler_params=pltpu.CompilerParams(vmem_limit_bytes=40 << 20),
        name="home",
    )(*parts, grid_tokens, wm, wp)


TILE = 256
KEYS = 4096
STEP = 512


def self_kernel(wire_ref, out_ref, keys, values, scores, best):
    step = pl.program_id(0)
    tiles = KEYS // TILE

    @pl.when(step == 0)
    def _():
        low = low_lanes(SEG)
        for s in range(16):
            keys[pl.ds(s * 256, 256), :] = wire_ref[s, pl.ds(0, 256), :]
            packed = wire_ref[s, pl.ds(256, SEG), :].astype(F32)
            values[pl.ds(s * 256, SEG), :] = jnp.where(low, packed, 1.0).astype(BF)
            values[pl.ds(s * 256 + SEG, SEG), :] = jnp.where(
                low, pltpu.roll(packed, 64, 1), 1.0
            ).astype(BF)

    low = low_lanes(TILE)

    def scores_of(into):
        tile = jnp.minimum(step, tiles - 1)
        qk = wire_ref[tile, pl.ds(0, TILE), :].astype(F32)
        q = jnp.where(low, 0.0, pltpu.roll(qk, 64, 1)).astype(BF)
        run = jnp.full((TILE, 128), DEAD * 1e8, F32)
        for k in range(KEYS // STEP):
            s = lax.dot_general(
                q,
                keys[pl.ds(k * STEP, STEP), :],
                (((1,), (1,)), ((), ())),
                preferred_element_type=F32,
            )
            scores[into, :, pl.ds(k * STEP, STEP)] = s
            for i in range(STEP // 128):
                run = jnp.maximum(run, s[:, i * 128 : (i + 1) * 128])
            yield
        best[into] = jnp.broadcast_to(jnp.max(run, axis=-1, keepdims=True), (TILE, 128))

    def output_of(source):
        m = best[source][:, :1]
        total = jnp.zeros((TILE, 128), F32)
        for k in range(KEYS // STEP):
            s = scores[source, :, pl.ds(k * STEP, STEP)]
            p = jnp.exp2((s - m) * SCALE).astype(BF)
            total += jnp.dot(p, values[pl.ds(k * STEP, STEP), :], preferred_element_type=F32)
            yield
        o = (total / pltpu.roll(total, 64, 1))
        half = low_lanes(SEG)
        out_ref[0] = jnp.where(half, o[:SEG], pltpu.roll(o[SEG:], 64, 1)).astype(BF)

    now, before = step % 2, (step + 1) % 2
    jobs = [scores_of(now), output_of(before)]
    while jobs:
        for job in list(jobs):
            try:
                next(job)
            except StopIteration:
                jobs.remove(job)


def self_call(wire):
    tiles = KEYS // TILE
    return pl.pallas_call(
        self_kernel,
        grid=(tiles + 1,),
        out_shape=jax.ShapeDtypeStruct((tiles, SEG, 128), BF),
        in_specs=[pl.BlockSpec((16, 3 * SEG, 128), lambda i: (0, 0, 0))],
        out_specs=pl.BlockSpec((1, SEG, 128), lambda i: (jnp.maximum(i - 1, 0), 0, 0)),
        scratch_shapes=[
            pltpu.VMEM((KEYS, 128), BF),
            pltpu.VMEM((KEYS, 128), BF),
            pltpu.VMEM((2, TILE, KEYS), F32),
            pltpu.VMEM((2, TILE, 128), F32),
        ],
        compiler_params=pltpu.CompilerParams(vmem_limit_bytes=40 << 20),
        name="self_attention",
    )(wire)


def final_kernel(wire_ref, mixed_ref, w_ref, out_ref):
    low = low_lanes(SEG)
    tops, bottoms = [], []
    for hp in range(PAIRS):
        one = wire_ref[2 * hp].astype(F32)
        two = wire_ref[2 * hp + 1].astype(F32)
        tops.append(jnp.where(low, one, pltpu.roll(two, 64, 1)).astype(BF))
        bottoms.append(jnp.where(low, pltpu.roll(one, 64, 1), two).astype(BF))
    attended = jnp.concatenate(
        [jnp.concatenate(tops, axis=1), jnp.concatenate(bottoms, axis=1)], axis=0
    )
    out_ref[...] = (
        mixed_ref[...].astype(F32) + jnp.dot(attended, w_ref[...], preferred_element_type=F32)
    ).astype(BF)


def final_call(wire, mixed, w):
    return pl.pallas_call(
        final_kernel,
        out_shape=jax.ShapeDtypeStruct((2 * SEG, D), BF),
        in_specs=[VMEM] * 3,
        out_specs=VMEM,
        compiler_params=pltpu.CompilerParams(vmem_limit_bytes=24 << 20),
        name="final",
    )(wire, mixed, w)


def on_device(
    scan_tokens,
    grid_tokens,
    seg_slot,
    segment_lists,
    query_weight,
    key_weight,
    value_weight,
    mixer_weight,
    packed_weight,
    merged_weight,
):
    shape = (lax.axis_size("region"), 4, 4)
    region = lax.axis_index("region")
    seq = lax.axis_index("seq")
    z, x = seq // 4, seq % 4
    even = region % 2 == 0
    a = jnp.where(even, z, x)
    b = jnp.where(even, x, z)

    def move(value, tokens_ring, step):
        return lax.ppermute(value, AX, ring(shape, tokens_ring, step))

    half = scan_tokens.shape[0] // 2
    upper, lower = scan_tokens[:half], scan_tokens[half:]
    up_a = move(upper, True, 1)
    down_b = move(lower, True, -1)
    up_b = move(lower, True, 1)
    down_a = move(upper, True, -1)
    far_a = move(up_a, True, 1)
    far_b = move(down_b, True, -1)

    queries = jnp.dot(normed(grid_tokens), query_weight, preferred_element_type=F32).astype(BF)
    peers = [queries] + [move(queries, False, -p) for p in (1, 2, 3)]

    row = jnp.concatenate(
        [seg_slot, segment_lists.reshape(-1), jnp.zeros((104,), jnp.int32)]
    ).reshape(1, 128)
    meta = lax.all_to_all(
        jnp.broadcast_to(row, (shape[0] * 16, 128)), AX, 0, 0, tiled=True
    )
    plan = make_plan(jnp.stack([region, a, b]).astype(jnp.int32), meta)

    state = cross_call(
        plan,
        peers,
        (0, 1, 3),
        [[scan_tokens], [down_a, down_b], [up_a, up_b]],
        key_weight,
        value_weight,
    )
    partial = cross_call(
        plan, peers, (2,), [[far_a, far_b]], key_weight, value_weight, state
    )
    back = [partial[0]] + [move(partial[p], False, p) for p in (1, 2, 3)]
    mixed, wire = home_call(back, grid_tokens, mixer_weight, packed_weight)
    regional = lax.all_to_all(wire, "seq", split_axis=0, concat_axis=0, tiled=True)
    attended = self_call(regional)
    returned = lax.all_to_all(attended, "seq", split_axis=0, concat_axis=0, tiled=True)
    return final_call(returned, mixed, merged_weight)


def solution(mesh):
    in_specs = (
        P(AX, None),
        P(AX, None),
        P(AX),
        P(AX, None),
        P(),
        P(),
        P(),
        P(),
        P(),
        P(),
    )
    return jax.shard_map(
        on_device, mesh=mesh, in_specs=in_specs, out_specs=P(AX, None), check_vma=False
    )
```
